32 devices in a mesh: dp: 4 (over z), tensor: 8 (over y, x, core).
Axes of the slice: x: 2, y: 2, z: 4, core: 2. Of those that a mesh axis runs over, the one named last changes fastest.
Arguments:
- gradients: bfloat16 [4, 64, 512, 512], P('dp', None, 'tensor'), may hold values from -240 to 240
- momentum: bfloat16 [4, 32, 512, 512], P('dp', None, 'tensor'), may hold values from -36 to 36
- owners: int32 [64], replicated, may hold values from 0 to 3, as said below
Outputs:
- updates: float32 [4, 32, 512, 512], P('dp', None, 'tensor')
The draws below stay inside these ranges and needn't reach their ends.
Inputs may be any that keep to these rules, and one draw needn't show every extreme that they name: `owners`: the blocks b with b // 16 == h give at most 8 blocks to any one owner, and exactly 8 to some owner, for every h; each owner holds at most 32 blocks, and some owner holds exactly 32.
All inputs are finite; a program needn't handle non-finite values.
Results may differ from the reference program's by a relative error of at most 0.018.
Values may be sent and summed in bfloat16 or wider, within the bound.
A program may use at most 64 MiB of HBM per device.

```python
import math
import jax
import jax.numpy as jnp
from jax import lax

BLOCK = 512
BPD = 16
ITERS = 3
NB = 64
PAIR = 8
MOST = 32
N_DP = 4


def draw_gradients(key, part):
    folded = jax.random.fold_in(key, 11)
    row_key, col_key, own_key = jax.random.split(folded, 3)
    row_scale = jnp.exp(jax.random.uniform(row_key, (NB, BLOCK, 1), jnp.float32, 0.0, math.log(10.0)))
    col_scale = jnp.exp(jax.random.uniform(col_key, (NB, 1, BLOCK), jnp.float32, 0.0, math.log(10.0)))
    replica_ids = jnp.arange(N_DP, dtype=jnp.int32)[:, None]
    holder_ids = (jnp.arange(NB, dtype=jnp.int32) // BPD)[None, :]
    boost = jnp.where(replica_ids == holder_ids, 6.0, 1.0).astype(jnp.float32)[:, :, None, None]
    blended = jax.random.truncated_normal(own_key, -4.0, 4.0, (N_DP, NB, BLOCK, BLOCK), jnp.float32) * boost
    return (0.1 * blended * row_scale[None] * col_scale[None]).astype(jnp.bfloat16)


def draw_owners(key, part):
    folded = jax.random.fold_in(key, 5)
    busiest = jax.random.randint(jax.random.fold_in(folded, 1), (), 0, N_DP).astype(jnp.int32)

    def one_group(group_key):
        pick_key, mix_key = jax.random.split(group_key)
        tickets = jax.random.permutation(pick_key, (N_DP - 1) * PAIR)[:BPD - PAIR].astype(jnp.int32)
        others = tickets // PAIR
        others = others + (others >= busiest).astype(jnp.int32)
        assigned = jnp.concatenate([jnp.full((PAIR,), busiest, jnp.int32), others.astype(jnp.int32)])
        return assigned[jax.random.permutation(mix_key, BPD)]
    group_keys = jax.random.split(jax.random.fold_in(folded, 2), N_DP)
    return jax.vmap(one_group)(group_keys).reshape(NB).astype(jnp.int32)


def shard_levels(key, extent, shards, smallest, top_value):
    factor_of, own = 1.0, jax.random.fold_in(key, 6)
    for dim, parts in shards:
        draws = jnp.exp(jax.random.uniform(jax.random.fold_in(own, dim), (parts,), jnp.float32, smallest / len(shards), top_value / len(shards)))
        factor_of = factor_of * jnp.repeat(draws, extent[dim] // parts).reshape([-1 if axis == dim else 1 for axis in range(len(extent))])
    return factor_of


def centred(stream_key, shape, deviation, most, cuts=(), kind=jnp.bfloat16):
    result = deviation * jax.random.normal(stream_key, shape, jnp.float32)
    if cuts:
        result = result * shard_levels(stream_key, shape, cuts, -0.22, 0.18)
    return jnp.clip(result, -most, most).astype(kind)


def setup_inputs(seed: int = 0) -> dict:
    arg_keys = jax.random.split(jax.random.key(seed), 4)
    gradients = draw_gradients(jax.random.fold_in(arg_keys[3], 71), 0)
    momentum = centred(arg_keys[1], (N_DP, MOST, BLOCK, BLOCK), 6.0, 36.0, ((0, 4), (2, 8)))
    owners = draw_owners(jax.random.fold_in(arg_keys[3], 71), 0)
    return {"gradients": gradients, "momentum": momentum, "owners": owners}


decay_rate = 0.95
newton_a = 3.4445
newton_b = -4.775
newton_c = 2.0315
norm_eps = 1e-07

def ranks_of(labels):
    length = labels.shape[0]
    places = jnp.arange(length, dtype=jnp.int32)
    earlier = (labels[None, :] == labels[:, None]) & (places[None, :] < places[:, None])
    return lax.optimization_barrier(jnp.sum(earlier.astype(jnp.int32), axis=1)).astype(jnp.int32)

def iterate_block(blended):
    widened = blended.astype(jnp.float32)
    length_sq = jnp.sum(widened * widened)
    current = widened / (jnp.sqrt(length_sq) + norm_eps)
    scale_up = math.sqrt(BLOCK)
    highest = lax.Precision.HIGHEST
    for iteration in range(ITERS):
        squared = jnp.dot(current, current.T, precision=highest, preferred_element_type=jnp.float32)
        polynomial = newton_b * squared + newton_c * jnp.dot(squared, squared, precision=highest, preferred_element_type=jnp.float32)
        current = newton_a * current + jnp.dot(polynomial, current, precision=highest, preferred_element_type=jnp.float32)
    return current * scale_up

def reference(gradients, momentum, owners):
    accumulated = gradients[0].astype(jnp.float32)
    for replica in range(1, N_DP):
        accumulated = accumulated + gradients[replica].astype(jnp.float32)
    summed = accumulated.astype(jnp.bfloat16)
    slot_rank = ranks_of(owners)

    def one_block(block_id):
        widened_g = summed[block_id].astype(jnp.float32)
        widened_m = momentum[owners[block_id], slot_rank[block_id]].astype(jnp.float32)
        blended = (widened_g + decay_rate * (decay_rate * widened_m + widened_g)).astype(jnp.bfloat16)
        return iterate_block(blended)
    finished = lax.map(one_block, jnp.arange(NB, dtype=jnp.int32))
    empty = jnp.zeros((N_DP, MOST, BLOCK, BLOCK), jnp.float32)
    return empty.at[owners, slot_rank].set(finished)
```

```python
import math

import jax
import jax.numpy as jnp
from jax import lax
from jax.sharding import PartitionSpec as P

ITERS = 3


decay_rate = 0.95
newton_a = 3.4445
newton_b = -4.775
newton_c = 2.0315
norm_eps = 1e-07


def ranks_of(labels):
    length = labels.shape[0]
    places = jnp.arange(length, dtype=jnp.int32)
    earlier = (labels[None, :] == labels[:, None]) & (places[None, :] < places[:, None])
    return jnp.sum(earlier.astype(jnp.int32), axis=1)


def dot(spec, left, right):
    return jnp.einsum(
        spec,
        left.astype(jnp.bfloat16),
        right.astype(jnp.bfloat16),
        preferred_element_type=jnp.float32,
    )


def iterate(blocks):
    widened = blocks.astype(jnp.float32) * (1.0 + decay_rate)
    lengths = jnp.sqrt(jnp.sum(widened * widened, axis=(1, 2), keepdims=True)) + norm_eps
    current = widened / lengths
    scale_up = math.sqrt(blocks.shape[1])
    for iteration in range(ITERS):
        squared = dot("kij,klj->kil", current, current)
        polynomial = newton_b * squared + newton_c * dot("kij,kjl->kil", squared, squared)
        current = newton_a * current + dot("kij,kjl->kil", polynomial, current)
    return current * scale_up


def body(gradients, momentum, owners):
    dp_count = lax.axis_size("dp")
    tp_count = lax.axis_size("tensor")
    my_group = lax.axis_index("dp")
    pieces = gradients[0]
    blocks_all, rows, columns = pieces.shape
    per_group = blocks_all // dp_count
    capacity = momentum.shape[1]
    slot_rank = ranks_of(owners)
    places = jnp.arange(blocks_all, dtype=jnp.int32)

    mine = owners == my_group
    moment = jnp.take(momentum[0], jnp.minimum(slot_rank, capacity - 1), axis=0)
    moment = jnp.where(mine[:, None, None], moment, jnp.zeros_like(moment)).astype(jnp.float32)
    ratio = decay_rate * decay_rate / (1.0 + decay_rate)
    folded = (pieces.astype(jnp.float32) + ratio * moment).astype(jnp.bfloat16)
    held = lax.psum_scatter(folded, "dp", scatter_dimension=0, tiled=True)

    per_device = (per_group + tp_count - 1) // tp_count
    padded_count = per_device * tp_count
    padded = jnp.pad(held, ((0, padded_count - per_group), (0, 0), (0, 0)))
    whole = lax.all_to_all(padded, "tensor", split_axis=0, concat_axis=1, tiled=True)
    finished = iterate(whole).astype(jnp.bfloat16)
    result = lax.all_to_all(finished, "tensor", split_axis=1, concat_axis=0, tiled=True)

    groups = jnp.arange(dp_count, dtype=jnp.int32)
    pair_most = (2 * per_group + dp_count - 1) // dp_count
    held_owner = lax.dynamic_slice_in_dim(owners, my_group * per_group, per_group)
    held_rank = ranks_of(held_owner)
    held_places = jnp.arange(per_group, dtype=jnp.int32)
    pair_ids = jnp.arange(pair_most, dtype=jnp.int32)
    matched = (held_owner[:, None, None] == groups[None, :, None]) & (
        held_rank[:, None, None] == pair_ids[None, None, :]
    )
    source = jnp.sum(jnp.where(matched, held_places[:, None, None], 0), axis=0).reshape(-1)
    outgoing = jnp.take(result, source, axis=0)
    outgoing = outgoing.reshape(dp_count, pair_most, rows, columns)
    incoming = lax.all_to_all(outgoing, "dp", split_axis=0, concat_axis=0, tiled=True)
    incoming = incoming.reshape(dp_count * pair_most, rows, columns)
    group_rank = ranks_of(owners * dp_count + places // per_group)
    position = places // per_group * pair_most + group_rank
    slot_ids = jnp.arange(capacity, dtype=jnp.int32)
    my_slots = mine[:, None] & (slot_rank[:, None] == slot_ids[None, :])
    occupied = jnp.any(my_slots, axis=0)
    arriving = jnp.sum(jnp.where(my_slots, position[:, None], 0), axis=0)
    chosen = jnp.take(incoming, arriving, axis=0).astype(jnp.float32)
    update = jnp.where(occupied[:, None, None], chosen, jnp.zeros_like(chosen))
    return update[None]


def solution(mesh):
    in_specs = (P("dp", None, "tensor", None), P("dp", None, "tensor", None), P())
    out_specs = P("dp", None, "tensor", None)
    return jax.shard_map(body, mesh=mesh, in_specs=in_specs, out_specs=out_specs, check_vma=False)
```

```python
import functools
import math

import jax
import jax.numpy as jnp
from jax import lax
from jax.experimental import pallas as pl
from jax.experimental.pallas import tpu as pltpu
from jax.sharding import PartitionSpec as P

ITERS = 3


decay_rate = 0.95
newton_a = 3.4445
newton_b = -4.775
newton_c = 2.0315
norm_eps = 1e-07


def ranks_of(labels):
    length = labels.shape[0]
    places = jnp.arange(length, dtype=jnp.int32)
    earlier = (labels[None, :] == labels[:, None]) & (places[None, :] < places[:, None])
    return jnp.sum(earlier.astype(jnp.int32), axis=1)


def dot(spec, left, right):
    return jnp.einsum(
        spec,
        left.astype(jnp.bfloat16),
        right.astype(jnp.bfloat16),
        preferred_element_type=jnp.float32,
    )


def iterate(blocks):
    widened = blocks.astype(jnp.float32) * (1.0 + decay_rate)
    lengths = jnp.sqrt(jnp.sum(widened * widened, axis=(1, 2), keepdims=True)) + norm_eps
    current = widened / lengths
    scale_up = math.sqrt(blocks.shape[1])
    for iteration in range(ITERS):
        squared = dot("kij,klj->kil", current, current)
        polynomial = newton_b * squared + newton_c * dot("kij,kjl->kil", squared, squared)
        current = newton_a * current + dot("kij,kjl->kil", polynomial, current)
    return current * scale_up


def body(gradients, momentum, owners):
    dp_count = lax.axis_size("dp")
    tp_count = lax.axis_size("tensor")
    my_group = lax.axis_index("dp")
    pieces = gradients[0]
    blocks_all, rows, columns = pieces.shape
    per_group = blocks_all // dp_count
    capacity = momentum.shape[1]
    slot_rank = ranks_of(owners)
    places = jnp.arange(blocks_all, dtype=jnp.int32)

    mine = owners == my_group
    moment = jnp.take(momentum[0], jnp.minimum(slot_rank, capacity - 1), axis=0)
    moment = jnp.where(mine[:, None, None], moment, jnp.zeros_like(moment)).astype(jnp.float32)
    ratio = decay_rate * decay_rate / (1.0 + decay_rate)
    folded = (pieces.astype(jnp.float32) + ratio * moment).astype(jnp.bfloat16)
    held = lax.psum_scatter(folded, "dp", scatter_dimension=0, tiled=True)

    per_device = (per_group + tp_count - 1) // tp_count
    padded_count = per_device * tp_count
    padded = jnp.pad(held, ((0, padded_count - per_group), (0, 0), (0, 0)))
    whole = lax.all_to_all(padded, "tensor", split_axis=0, concat_axis=1, tiled=True)
    finished = iterate(whole).astype(jnp.bfloat16)
    result = lax.all_to_all(finished, "tensor", split_axis=1, concat_axis=0, tiled=True)

    groups = jnp.arange(dp_count, dtype=jnp.int32)
    pair_most = (2 * per_group + dp_count - 1) // dp_count
    held_owner = lax.dynamic_slice_in_dim(owners, my_group * per_group, per_group)
    held_rank = ranks_of(held_owner)
    held_places = jnp.arange(per_group, dtype=jnp.int32)
    pair_ids = jnp.arange(pair_most, dtype=jnp.int32)
    matched = (held_owner[:, None, None] == groups[None, :, None]) & (
        held_rank[:, None, None] == pair_ids[None, None, :]
    )
    source = jnp.sum(jnp.where(matched, held_places[:, None, None], 0), axis=0).reshape(-1)
    outgoing = jnp.take(result, source, axis=0)
    outgoing = outgoing.reshape(dp_count, pair_most, rows, columns)
    incoming = lax.all_to_all(outgoing, "dp", split_axis=0, concat_axis=0, tiled=True)
    incoming = incoming.reshape(dp_count * pair_most, rows, columns)
    group_rank = ranks_of(owners * dp_count + places // per_group)
    position = places // per_group * pair_most + group_rank
    slot_ids = jnp.arange(capacity, dtype=jnp.int32)
    my_slots = mine[:, None] & (slot_rank[:, None] == slot_ids[None, :])
    occupied = jnp.any(my_slots, axis=0)
    arriving = jnp.sum(jnp.where(my_slots, position[:, None], 0), axis=0)
    chosen = jnp.take(incoming, arriving, axis=0).astype(jnp.float32)
    update = jnp.where(occupied[:, None, None], chosen, jnp.zeros_like(chosen))
    return update[None]


MESH = pl.DeviceIdType.MESH


def kernel(
    sizes, weight, slot, g_ref, m_ref, out_ref,
    arrived, partial, whole, ready, gathered, current,
    chain_send, chain_recv, scatter_send, scatter_recv, return_send, ahead_send, gather_recv, out_sem,
):
    n, width, half, rows, lead = sizes
    columns = g_ref.shape[2]
    z, t = lax.axis_index("dp"), lax.axis_index("tensor")
    per_device = half // width
    is_end = (z == 0) | (z == n - 1)
    low = 2 * z < n - 1

    barrier = pltpu.get_barrier_semaphore()

    @pl.when(z > 0)
    def _():
        pl.semaphore_signal(barrier, inc=1, device_id=(z - 1, t), device_id_type=MESH)

    @pl.when(z < n - 1)
    def _():
        pl.semaphore_signal(barrier, inc=1, device_id=(z + 1, t), device_id_type=MESH)

    def greet(k, carry):
        peer = lax.rem(t + k, width)
        pl.semaphore_signal(barrier, inc=1, device_id=(z, peer), device_id_type=MESH)
        return carry

    lax.fori_loop(1, width, greet, 0)
    pl.semaphore_wait(barrier, jnp.where(is_end, width, width + 1))

    def chain_copy(d, c):
        return pltpu.make_async_remote_copy(
            src_ref=partial.at[d, c],
            dst_ref=arrived.at[d, c],
            send_sem=chain_send.at[d, c],
            recv_sem=chain_recv.at[d, c],
            device_id=(z + 2 * d - 1, t),
            device_id_type=MESH,
        )

    def own(d, c):
        block = d * half + c
        moment = m_ref[slot[block]].astype(jnp.float32)
        return g_ref[block].astype(jnp.float32) + weight[block] * moment

    def my_rows(place):
        return pl.ds(pl.multiple_of(place * rows, rows), rows)

    def start_chain(d, c):
        partial[d, c] = own(d, c).astype(jnp.bfloat16)
        chain_copy(d, c).start()

    def add_chain(d, c):
        chain_copy(d, c).wait_recv()
        total = own(d, c) + arrived[d, c].astype(jnp.float32)
        partial[d, c] = total.astype(jnp.bfloat16)

    def scatter_copy(d, c, peer, sem):
        return pltpu.make_async_remote_copy(
            src_ref=partial.at[d, c],
            dst_ref=whole.at[c // width, my_rows(t)],
            send_sem=scatter_send.at[c],
            recv_sem=sem,
            device_id=(z, peer),
            device_id_type=MESH,
        )

    def return_copy(d, j, peer):
        block = d * half + j * width + t
        return pltpu.make_async_remote_copy(
            src_ref=ready.at[j, my_rows(peer)],
            dst_ref=gathered.at[block],
            send_sem=return_send.at[j, peer],
            recv_sem=gather_recv.at[block],
            device_id=(z, peer),
            device_id_type=MESH,
        )

    def ahead_copy(d, c):
        block = d * half + c
        return pltpu.make_async_remote_copy(
            src_ref=gathered.at[block],
            dst_ref=gathered.at[block],
            send_sem=ahead_send.at[block],
            recv_sem=gather_recv.at[block],
            device_id=(z + 1 - 2 * d, t),
            device_id_type=MESH,
        )

    def iterate_in(j):
        widened = whole[j].astype(jnp.float32) * (1.0 + decay_rate)
        length = jnp.sqrt(jnp.sum(widened * widened)) + norm_eps
        current[...] = widened / length

        def once(k, carry):
            now = current[...]
            low_now = now.astype(jnp.bfloat16)
            squared = lax.dot_general(
                low_now, low_now, (((1,), (1,)), ((), ())), preferred_element_type=jnp.float32
            )
            low_squared = squared.astype(jnp.bfloat16)
            polynomial = newton_b * squared + newton_c * jnp.dot(
                low_squared, low_squared, preferred_element_type=jnp.float32
            )
            current[...] = newton_a * now + jnp.dot(
                polynomial.astype(jnp.bfloat16), low_now, preferred_element_type=jnp.float32
            )
            return carry

        lax.fori_loop(0, ITERS, once, 0)
        ready[j] = (current[...] * math.sqrt(columns)).astype(jnp.bfloat16)

    @pl.when(is_end)
    def _():
        near = jnp.where(z == 0, 0, 1)
        far = 1 - near

        def begin(c, carry):
            start_chain(far, c)
            return carry

        lax.fori_loop(0, half, begin, 0)

        def block_step(j, carry):
            def chunk(k, inner):
                c = j * width + k
                add_chain(near, c)

                @pl.when(k == t)
                def _():
                    pltpu.make_async_copy(
                        partial.at[near, c], whole.at[j, my_rows(t)], scatter_recv.at[j, t]
                    ).start()

                @pl.when(k != t)
                def _():
                    scatter_copy(near, c, k, scatter_recv.at[j, t]).start()

                return inner

            lax.fori_loop(0, width, chunk, 0)

            def land(k, inner):
                pltpu.make_async_copy(
                    partial.at[near, 0], whole.at[j, my_rows(k)], scatter_recv.at[j, k]
                ).wait()
                return inner

            lax.fori_loop(0, width, land, 0)
            iterate_in(j)

            def give(k, inner):
                @pl.when(k == t)
                def _():
                    block = near * half + j * width + t
                    pltpu.make_async_copy(
                        ready.at[j, my_rows(t)], gathered.at[block], gather_recv.at[block]
                    ).start()

                @pl.when(k != t)
                def _():
                    return_copy(near, j, k).start()

                return inner

            lax.fori_loop(0, width, give, 0)
            return carry

        lax.fori_loop(0, per_device, block_step, 0)

    @pl.when(jnp.logical_not(is_end))
    def _():
        early = jnp.where(low, 1, 0)

        def forward(d, c):
            add_chain(d, c)
            chain_copy(d, c).start()

        def step(i, carry):
            @pl.when(i < half)
            def _():
                forward(early, i)

            @pl.when(i >= lead)
            def _():
                forward(1 - early, i - lead)

            return carry

        lax.fori_loop(0, half + lead, step, 0)

    def pass_on(d, c):
        ahead_copy(d, c).wait_recv()

        @pl.when((z + 1 - 2 * d >= 0) & (z + 1 - 2 * d < n))
        def _():
            ahead_copy(d, c).start()

    first = jnp.where(low, 0, 1)
    delay = jnp.where(is_end, half, lead)

    def gather_step(i, carry):
        @pl.when(i < half)
        def _():
            pass_on(first, i)

        @pl.when(i >= delay)
        def _():
            pass_on(1 - first, i - delay)

        return carry

    lax.fori_loop(0, half + delay, gather_step, 0)
    final = pltpu.make_async_copy(gathered, out_ref, out_sem)
    final.start()

    for d in range(2):
        sink = 0 if d == 0 else n - 1

        def settle(c, carry):
            @pl.when(z != sink)
            def _():
                chain_copy(d, c).wait_send()

            @pl.when(z != n - 1 - sink)
            def _():
                ahead_copy(d, c).wait_send()

            @pl.when((z == sink) & (lax.rem(c, width) != t))
            def _():
                scatter_copy(d, c, lax.rem(c, width), scatter_recv.at[0, 0]).wait_send()
                return_copy(d, c // width, lax.rem(c, width)).wait_send()

            return carry

        lax.fori_loop(0, half, settle, 0)
    final.wait()


def pick_kernel(index, filled, in_ref, out_ref):
    place = pl.program_id(0)
    piece = in_ref[0].astype(jnp.float32)
    out_ref[0, 0] = jnp.where(filled[place] > 0, piece, jnp.zeros_like(piece))


def fused(gradients, momentum, owners):
    n = lax.axis_size("dp")
    width = lax.axis_size("tensor")
    me = lax.axis_index("dp")
    pieces = gradients[0]
    blocks_all, rows, columns = pieces.shape
    capacity = momentum.shape[1]
    half = blocks_all // 2
    lead = min(4, half)
    slot_rank = ranks_of(owners)
    mine = owners == me
    ratio = decay_rate * decay_rate / (1.0 + decay_rate)
    weight = jnp.where(mine, ratio, 0.0).astype(jnp.float32)
    slot = jnp.minimum(slot_rank, capacity - 1)
    order = columns
    low = jnp.bfloat16
    all_results = pl.pallas_call(
        functools.partial(kernel, (n, width, half, rows, lead)),
        out_shape=jax.ShapeDtypeStruct((blocks_all, rows, columns), low),
        in_specs=[
            pl.BlockSpec(memory_space=pltpu.SMEM),
            pl.BlockSpec(memory_space=pltpu.SMEM),
            pl.BlockSpec(memory_space=pltpu.VMEM),
            pl.BlockSpec(memory_space=pltpu.VMEM),
        ],
        out_specs=pl.BlockSpec(memory_space=pl.ANY),
        scratch_shapes=[
            pltpu.VMEM((2, half, rows, columns), low),
            pltpu.VMEM((2, half, rows, columns), low),
            pltpu.VMEM((half // width, order, columns), low),
            pltpu.VMEM((half // width, order, columns), low),
            pltpu.VMEM((blocks_all, rows, columns), low),
            pltpu.VMEM((order, columns), jnp.float32),
            pltpu.SemaphoreType.DMA((2, half)),
            pltpu.SemaphoreType.DMA((2, half)),
            pltpu.SemaphoreType.DMA((half,)),
            pltpu.SemaphoreType.DMA((half // width, width)),
            pltpu.SemaphoreType.DMA((half // width, width)),
            pltpu.SemaphoreType.DMA((blocks_all,)),
            pltpu.SemaphoreType.DMA((blocks_all,)),
            pltpu.SemaphoreType.DMA,
        ],
        compiler_params=pltpu.CompilerParams(
            collective_id=0, has_side_effects=True, vmem_limit_bytes=50 * 1024 * 1024
        ),
        name="muon_chain",
    )(weight, slot, pieces, momentum[0])

    slot_ids = jnp.arange(capacity, dtype=jnp.int32)
    places = jnp.arange(blocks_all, dtype=jnp.int32)
    my_slots = mine[:, None] & (slot_rank[:, None] == slot_ids[None, :])
    filled = jnp.any(my_slots, axis=0).astype(jnp.int32)
    index = jnp.sum(jnp.where(my_slots, places[:, None], 0), axis=0)
    return pl.pallas_call(
        pick_kernel,
        out_shape=jax.ShapeDtypeStruct((1, capacity, rows, columns), jnp.float32),
        grid_spec=pltpu.PrefetchScalarGridSpec(
            num_scalar_prefetch=2,
            grid=(capacity,),
            in_specs=[pl.BlockSpec((1, rows, columns), lambda s, index, filled: (index[s], 0, 0))],
            out_specs=pl.BlockSpec((1, 1, rows, columns), lambda s, index, filled: (0, s, 0, 0)),
        ),
        name="muon_pick",
    )(index, filled, all_results)


def choose(gradients, momentum, owners):
    n, width = lax.axis_size("dp"), lax.axis_size("tensor")
    blocks_all = gradients.shape[1]
    if n > 1 and blocks_all % (2 * width) == 0 and gradients.shape[2] % 16 == 0:
        return fused(gradients, momentum, owners)
    return body(gradients, momentum, owners)


def solution(mesh):
    in_specs = (P("dp", None, "tensor", None), P("dp", None, "tensor", None), P())
    out_specs = P("dp", None, "tensor", None)
    return jax.shard_map(choose, mesh=mesh, in_specs=in_specs, out_specs=out_specs, check_vma=False)
```

```python
import functools
import math

import jax
import jax.numpy as jnp
from jax import lax
from jax.experimental import pallas as pl
from jax.experimental.pallas import tpu as pltpu
from jax.sharding import PartitionSpec as P

ITERS = 3


decay_rate = 0.95
newton_a = 3.4445
newton_b = -4.775
newton_c = 2.0315
norm_eps = 1e-07


def ranks_of(labels):
    length = labels.shape[0]
    places = jnp.arange(length, dtype=jnp.int32)
    earlier = (labels[None, :] == labels[:, None]) & (places[None, :] < places[:, None])
    return jnp.sum(earlier.astype(jnp.int32), axis=1)


def dot(spec, left, right):
    return jnp.einsum(
        spec,
        left.astype(jnp.bfloat16),
        right.astype(jnp.bfloat16),
        preferred_element_type=jnp.float32,
    )


def iterate(blocks):
    widened = blocks.astype(jnp.float32) * (1.0 + decay_rate)
    lengths = jnp.sqrt(jnp.sum(widened * widened, axis=(1, 2), keepdims=True)) + norm_eps
    current = widened / lengths
    scale_up = math.sqrt(blocks.shape[1])
    for iteration in range(ITERS):
        squared = dot("kij,klj->kil", current, current)
        polynomial = newton_b * squared + newton_c * dot("kij,kjl->kil", squared, squared)
        current = newton_a * current + dot("kij,kjl->kil", polynomial, current)
    return current * scale_up


def body(gradients, momentum, owners):
    dp_count = lax.axis_size("dp")
    tp_count = lax.axis_size("tensor")
    my_group = lax.axis_index("dp")
    pieces = gradients[0]
    blocks_all, rows, columns = pieces.shape
    per_group = blocks_all // dp_count
    capacity = momentum.shape[1]
    slot_rank = ranks_of(owners)
    places = jnp.arange(blocks_all, dtype=jnp.int32)

    mine = owners == my_group
    moment = jnp.take(momentum[0], jnp.minimum(slot_rank, capacity - 1), axis=0)
    moment = jnp.where(mine[:, None, None], moment, jnp.zeros_like(moment)).astype(jnp.float32)
    ratio = decay_rate * decay_rate / (1.0 + decay_rate)
    folded = (pieces.astype(jnp.float32) + ratio * moment).astype(jnp.bfloat16)
    held = lax.psum_scatter(folded, "dp", scatter_dimension=0, tiled=True)

    per_device = (per_group + tp_count - 1) // tp_count
    padded_count = per_device * tp_count
    padded = jnp.pad(held, ((0, padded_count - per_group), (0, 0), (0, 0)))
    whole = lax.all_to_all(padded, "tensor", split_axis=0, concat_axis=1, tiled=True)
    finished = iterate(whole).astype(jnp.bfloat16)
    result = lax.all_to_all(finished, "tensor", split_axis=1, concat_axis=0, tiled=True)

    groups = jnp.arange(dp_count, dtype=jnp.int32)
    pair_most = (2 * per_group + dp_count - 1) // dp_count
    held_owner = lax.dynamic_slice_in_dim(owners, my_group * per_group, per_group)
    held_rank = ranks_of(held_owner)
    held_places = jnp.arange(per_group, dtype=jnp.int32)
    pair_ids = jnp.arange(pair_most, dtype=jnp.int32)
    matched = (held_owner[:, None, None] == groups[None, :, None]) & (
        held_rank[:, None, None] == pair_ids[None, None, :]
    )
    source = jnp.sum(jnp.where(matched, held_places[:, None, None], 0), axis=0).reshape(-1)
    outgoing = jnp.take(result, source, axis=0)
    outgoing = outgoing.reshape(dp_count, pair_most, rows, columns)
    incoming = lax.all_to_all(outgoing, "dp", split_axis=0, concat_axis=0, tiled=True)
    incoming = incoming.reshape(dp_count * pair_most, rows, columns)
    group_rank = ranks_of(owners * dp_count + places // per_group)
    position = places // per_group * pair_most + group_rank
    slot_ids = jnp.arange(capacity, dtype=jnp.int32)
    my_slots = mine[:, None] & (slot_rank[:, None] == slot_ids[None, :])
    occupied = jnp.any(my_slots, axis=0)
    arriving = jnp.sum(jnp.where(my_slots, position[:, None], 0), axis=0)
    chosen = jnp.take(incoming, arriving, axis=0).astype(jnp.float32)
    update = jnp.where(occupied[:, None, None], chosen, jnp.zeros_like(chosen))
    return update[None]


MESH = pl.DeviceIdType.MESH


def kernel(
    sizes, weight, slot, g_ref, m_ref, out_ref,
    arrived, partial, whole, ready, gathered, current,
    chain_send, chain_recv, scatter_send, scatter_recv, return_send, ahead_send, gather_recv, out_sem,
):
    n, width, half, rows, lead = sizes
    columns = g_ref.shape[2]
    z, t = lax.axis_index("dp"), lax.axis_index("tensor")
    per_device = half // width
    gap = half
    is_end = (z == 0) | (z == n - 1)
    low = 2 * z < n - 1

    barrier = pltpu.get_barrier_semaphore()

    @pl.when(z > 0)
    def _():
        pl.semaphore_signal(barrier, inc=1, device_id=(z - 1, t), device_id_type=MESH)

    @pl.when(z < n - 1)
    def _():
        pl.semaphore_signal(barrier, inc=1, device_id=(z + 1, t), device_id_type=MESH)

    def greet(k, carry):
        peer = lax.rem(t + k, width)
        pl.semaphore_signal(barrier, inc=1, device_id=(z, peer), device_id_type=MESH)
        return carry

    lax.fori_loop(1, width, greet, 0)
    pl.semaphore_wait(barrier, jnp.where(is_end, width, width + 1))

    def chain_copy(d, c):
        return pltpu.make_async_remote_copy(
            src_ref=partial.at[d, c],
            dst_ref=arrived.at[d, c],
            send_sem=chain_send.at[d, c],
            recv_sem=chain_recv.at[d, c],
            device_id=(z + 2 * d - 1, t),
            device_id_type=MESH,
        )

    def own(d, c):
        block = d * half + c
        moment = m_ref[slot[block]].astype(jnp.float32)
        return g_ref[block].astype(jnp.float32) + weight[block] * moment

    def my_rows(place):
        return pl.ds(pl.multiple_of(place * rows, rows), rows)

    def start_chain(d, c):
        partial[d, c] = own(d, c).astype(jnp.bfloat16)
        chain_copy(d, c).start()

    def add_chain(d, c):
        chain_copy(d, c).wait_recv()
        total = own(d, c) + arrived[d, c].astype(jnp.float32)
        partial[d, c] = total.astype(jnp.bfloat16)

    def scatter_copy(d, c, peer, sem):
        return pltpu.make_async_remote_copy(
            src_ref=partial.at[d, c],
            dst_ref=whole.at[c // width, my_rows(t)],
            send_sem=scatter_send.at[c],
            recv_sem=sem,
            device_id=(z, peer),
            device_id_type=MESH,
        )

    def return_copy(d, j, peer):
        block = d * half + j * width + t
        return pltpu.make_async_remote_copy(
            src_ref=ready.at[j, my_rows(peer)],
            dst_ref=gathered.at[block],
            send_sem=return_send.at[j, peer],
            recv_sem=gather_recv.at[block],
            device_id=(z, peer),
            device_id_type=MESH,
        )

    def ahead_copy(d, c):
        block = d * half + c
        return pltpu.make_async_remote_copy(
            src_ref=gathered.at[block],
            dst_ref=gathered.at[block],
            send_sem=ahead_send.at[block],
            recv_sem=gather_recv.at[block],
            device_id=(z + 1 - 2 * d, t),
            device_id_type=MESH,
        )

    def pass_on(d, c):
        ahead_copy(d, c).wait_recv()

        @pl.when((z + 1 - 2 * d >= 0) & (z + 1 - 2 * d < n))
        def _():
            ahead_copy(d, c).start()

    def iterate_in(j):
        widened = whole[j].astype(jnp.float32) * (1.0 + decay_rate)
        length = jnp.sqrt(jnp.sum(widened * widened)) + norm_eps
        current[...] = widened / length

        def once(k, carry):
            now = current[...]
            low_now = now.astype(jnp.bfloat16)
            squared = lax.dot_general(
                low_now, low_now, (((1,), (1,)), ((), ())), preferred_element_type=jnp.float32
            )
            low_squared = squared.astype(jnp.bfloat16)
            polynomial = newton_b * squared + newton_c * jnp.dot(
                low_squared, low_squared, preferred_element_type=jnp.float32
            )
            current[...] = newton_a * now + jnp.dot(
                polynomial.astype(jnp.bfloat16), low_now, preferred_element_type=jnp.float32
            )
            return carry

        lax.fori_loop(0, ITERS, once, 0)
        ready[j] = (current[...] * math.sqrt(columns)).astype(jnp.bfloat16)

    @pl.when(is_end)
    def _():
        near = jnp.where(z == 0, 0, 1)
        far = 1 - near

        def begin(c, carry):
            start_chain(far, c)
            return carry

        lax.fori_loop(0, half, begin, 0)

        def pass_group(j):
            def one(k, inner):
                pass_on(near, j * width + k)
                return inner

            lax.fori_loop(0, width, one, 0)

        def block_step(j, carry):
            def chunk(k, inner):
                c = j * width + k
                add_chain(near, c)

                @pl.when(k == t)
                def _():
                    pltpu.make_async_copy(
                        partial.at[near, c], whole.at[j, my_rows(t)], scatter_recv.at[j, t]
                    ).start()

                @pl.when(k != t)
                def _():
                    scatter_copy(near, c, k, scatter_recv.at[j, t]).start()

                return inner

            lax.fori_loop(0, width, chunk, 0)

            def land(k, inner):
                pltpu.make_async_copy(
                    partial.at[near, 0], whole.at[j, my_rows(k)], scatter_recv.at[j, k]
                ).wait()
                return inner

            lax.fori_loop(0, width, land, 0)

            @pl.when(j > 0)
            def _():
                pass_group(j - 1)

            iterate_in(j)

            def give(k, inner):
                @pl.when(k == t)
                def _():
                    block = near * half + j * width + t
                    pltpu.make_async_copy(
                        ready.at[j, my_rows(t)], gathered.at[block], gather_recv.at[block]
                    ).start()

                @pl.when(k != t)
                def _():
                    return_copy(near, j, k).start()

                return inner

            lax.fori_loop(0, width, give, 0)
            return carry

        lax.fori_loop(0, per_device, block_step, 0)
        pass_group(per_device - 1)

        def finish(c, carry):
            pass_on(far, c)
            return carry

        lax.fori_loop(0, half, finish, 0)

    @pl.when(jnp.logical_not(is_end))
    def _():
        early = jnp.where(low, 1, 0)

        def forward(d, c):
            add_chain(d, c)
            chain_copy(d, c).start()

        def step(i, carry):
            @pl.when(i < half)
            def _():
                forward(early, i)

            @pl.when((i >= lead) & (i < half + lead))
            def _():
                forward(1 - early, i - lead)

            @pl.when((i >= gap) & (i < half + gap))
            def _():
                pass_on(1 - early, i - gap)

            @pl.when(i >= gap + lead)
            def _():
                pass_on(early, i - gap - lead)

            return carry

        lax.fori_loop(0, half + gap + lead, step, 0)

    final = pltpu.make_async_copy(gathered, out_ref, out_sem)
    final.start()

    for d in range(2):
        sink = 0 if d == 0 else n - 1

        def settle(c, carry):
            @pl.when(z != sink)
            def _():
                chain_copy(d, c).wait_send()

            @pl.when(z != n - 1 - sink)
            def _():
                ahead_copy(d, c).wait_send()

            @pl.when((z == sink) & (lax.rem(c, width) != t))
            def _():
                scatter_copy(d, c, lax.rem(c, width), scatter_recv.at[0, 0]).wait_send()
                return_copy(d, c // width, lax.rem(c, width)).wait_send()

            return carry

        lax.fori_loop(0, half, settle, 0)
    final.wait()


def pick_kernel(group, index, filled, in_ref, out_ref):
    base = pl.program_id(0) * group
    for k in range(group):
        piece = in_ref[index[base + k]].astype(jnp.float32)
        out_ref[0, k] = jnp.where(filled[base + k] > 0, piece, jnp.zeros_like(piece))


def fused(gradients, momentum, owners):
    n = lax.axis_size("dp")
    width = lax.axis_size("tensor")
    me = lax.axis_index("dp")
    pieces = gradients[0]
    blocks_all, rows, columns = pieces.shape
    capacity = momentum.shape[1]
    half = blocks_all // 2
    lead = min(2, half)
    slot_rank = ranks_of(owners)
    mine = owners == me
    ratio = decay_rate * decay_rate / (1.0 + decay_rate)
    weight = jnp.where(mine, ratio, 0.0).astype(jnp.float32)
    slot = jnp.minimum(slot_rank, capacity - 1)
    order = columns
    low = jnp.bfloat16
    all_results = pl.pallas_call(
        functools.partial(kernel, (n, width, half, rows, lead)),
        out_shape=jax.ShapeDtypeStruct((blocks_all, rows, columns), low),
        in_specs=[
            pl.BlockSpec(memory_space=pltpu.SMEM),
            pl.BlockSpec(memory_space=pltpu.SMEM),
            pl.BlockSpec(memory_space=pltpu.VMEM),
            pl.BlockSpec(memory_space=pltpu.VMEM),
        ],
        out_specs=pl.BlockSpec(memory_space=pl.ANY),
        scratch_shapes=[
            pltpu.VMEM((2, half, rows, columns), low),
            pltpu.VMEM((2, half, rows, columns), low),
            pltpu.VMEM((half // width, order, columns), low),
            pltpu.VMEM((half // width, order, columns), low),
            pltpu.VMEM((blocks_all, rows, columns), low),
            pltpu.VMEM((order, columns), jnp.float32),
            pltpu.SemaphoreType.DMA((2, half)),
            pltpu.SemaphoreType.DMA((2, half)),
            pltpu.SemaphoreType.DMA((half,)),
            pltpu.SemaphoreType.DMA((half // width, width)),
            pltpu.SemaphoreType.DMA((half // width, width)),
            pltpu.SemaphoreType.DMA((blocks_all,)),
            pltpu.SemaphoreType.DMA((blocks_all,)),
            pltpu.SemaphoreType.DMA,
        ],
        compiler_params=pltpu.CompilerParams(
            collective_id=0, has_side_effects=True, vmem_limit_bytes=50 * 1024 * 1024
        ),
        name="muon_chain",
    )(weight, slot, pieces, momentum[0])

    slot_ids = jnp.arange(capacity, dtype=jnp.int32)
    places = jnp.arange(blocks_all, dtype=jnp.int32)
    my_slots = mine[:, None] & (slot_rank[:, None] == slot_ids[None, :])
    filled = jnp.any(my_slots, axis=0).astype(jnp.int32)
    index = jnp.sum(jnp.where(my_slots, places[:, None], 0), axis=0)
    group = math.gcd(capacity, 4)
    return pl.pallas_call(
        functools.partial(pick_kernel, group),
        out_shape=jax.ShapeDtypeStruct((1, capacity, rows, columns), jnp.float32),
        grid_spec=pltpu.PrefetchScalarGridSpec(
            num_scalar_prefetch=2,
            grid=(capacity // group,),
            in_specs=[pl.BlockSpec(memory_space=pltpu.VMEM)],
            out_specs=pl.BlockSpec((1, group, rows, columns), lambda s, index, filled: (0, s, 0, 0)),
        ),
        name="muon_pick",
    )(index, filled, all_results)


def choose(gradients, momentum, owners):
    n, width = lax.axis_size("dp"), lax.axis_size("tensor")
    blocks_all = gradients.shape[1]
    if n > 1 and blocks_all % (2 * width) == 0 and gradients.shape[2] % 16 == 0:
        return fused(gradients, momentum, owners)
    return body(gradients, momentum, owners)


def solution(mesh):
    in_specs = (P("dp", None, "tensor", None), P("dp", None, "tensor", None), P())
    out_specs = P("dp", None, "tensor", None)
    return jax.shard_map(choose, mesh=mesh, in_specs=in_specs, out_specs=out_specs, check_vma=False)
```

```python
import functools
import math

import jax
import jax.numpy as jnp
from jax import lax
from jax.experimental import pallas as pl
from jax.experimental.pallas import tpu as pltpu
from jax.sharding import PartitionSpec as P

ITERS = 3


decay_rate = 0.95
newton_a = 3.4445
newton_b = -4.775
newton_c = 2.0315
norm_eps = 1e-07


def ranks_of(labels):
    length = labels.shape[0]
    places = jnp.arange(length, dtype=jnp.int32)
    earlier = (labels[None, :] == labels[:, None]) & (places[None, :] < places[:, None])
    return jnp.sum(earlier.astype(jnp.int32), axis=1)


def dot(spec, left, right):
    return jnp.einsum(
        spec,
        left.astype(jnp.bfloat16),
        right.astype(jnp.bfloat16),
        preferred_element_type=jnp.float32,
    )


def iterate(blocks):
    widened = blocks.astype(jnp.float32) * (1.0 + decay_rate)
    lengths = jnp.sqrt(jnp.sum(widened * widened, axis=(1, 2), keepdims=True)) + norm_eps
    current = widened / lengths
    scale_up = math.sqrt(blocks.shape[1])
    for iteration in range(ITERS):
        squared = dot("kij,klj->kil", current, current)
        polynomial = newton_b * squared + newton_c * dot("kij,kjl->kil", squared, squared)
        current = newton_a * current + dot("kij,kjl->kil", polynomial, current)
    return current * scale_up


def body(gradients, momentum, owners):
    dp_count = lax.axis_size("dp")
    tp_count = lax.axis_size("tensor")
    my_group = lax.axis_index("dp")
    pieces = gradients[0]
    blocks_all, rows, columns = pieces.shape
    per_group = blocks_all // dp_count
    capacity = momentum.shape[1]
    slot_rank = ranks_of(owners)
    places = jnp.arange(blocks_all, dtype=jnp.int32)

    mine = owners == my_group
    moment = jnp.take(momentum[0], jnp.minimum(slot_rank, capacity - 1), axis=0)
    moment = jnp.where(mine[:, None, None], moment, jnp.zeros_like(moment)).astype(jnp.float32)
    ratio = decay_rate * decay_rate / (1.0 + decay_rate)
    folded = (pieces.astype(jnp.float32) + ratio * moment).astype(jnp.bfloat16)
    held = lax.psum_scatter(folded, "dp", scatter_dimension=0, tiled=True)

    per_device = (per_group + tp_count - 1) // tp_count
    padded_count = per_device * tp_count
    padded = jnp.pad(held, ((0, padded_count - per_group), (0, 0), (0, 0)))
    whole = lax.all_to_all(padded, "tensor", split_axis=0, concat_axis=1, tiled=True)
    finished = iterate(whole).astype(jnp.bfloat16)
    result = lax.all_to_all(finished, "tensor", split_axis=1, concat_axis=0, tiled=True)

    groups = jnp.arange(dp_count, dtype=jnp.int32)
    pair_most = (2 * per_group + dp_count - 1) // dp_count
    held_owner = lax.dynamic_slice_in_dim(owners, my_group * per_group, per_group)
    held_rank = ranks_of(held_owner)
    held_places = jnp.arange(per_group, dtype=jnp.int32)
    pair_ids = jnp.arange(pair_most, dtype=jnp.int32)
    matched = (held_owner[:, None, None] == groups[None, :, None]) & (
        held_rank[:, None, None] == pair_ids[None, None, :]
    )
    source = jnp.sum(jnp.where(matched, held_places[:, None, None], 0), axis=0).reshape(-1)
    outgoing = jnp.take(result, source, axis=0)
    outgoing = outgoing.reshape(dp_count, pair_most, rows, columns)
    incoming = lax.all_to_all(outgoing, "dp", split_axis=0, concat_axis=0, tiled=True)
    incoming = incoming.reshape(dp_count * pair_most, rows, columns)
    group_rank = ranks_of(owners * dp_count + places // per_group)
    position = places // per_group * pair_most + group_rank
    slot_ids = jnp.arange(capacity, dtype=jnp.int32)
    my_slots = mine[:, None] & (slot_rank[:, None] == slot_ids[None, :])
    occupied = jnp.any(my_slots, axis=0)
    arriving = jnp.sum(jnp.where(my_slots, position[:, None], 0), axis=0)
    chosen = jnp.take(incoming, arriving, axis=0).astype(jnp.float32)
    update = jnp.where(occupied[:, None, None], chosen, jnp.zeros_like(chosen))
    return update[None]


MESH = pl.DeviceIdType.MESH


def kernel(
    sizes, weight, slot, g_ref, m_ref, out_ref,
    arrived, partial, whole, ready, gathered, current,
    chain_send, chain_recv, scatter_send, scatter_recv, return_send, ahead_send, gather_recv, out_sem,
):
    n, width, half, rows, lead = sizes
    columns = g_ref.shape[2]
    z, t = lax.axis_index("dp"), lax.axis_index("tensor")
    per_device = half // width
    gap = half
    is_end = (z == 0) | (z == n - 1)
    low = 2 * z < n - 1

    barrier = pltpu.get_barrier_semaphore()

    @pl.when(z > 0)
    def _():
        pl.semaphore_signal(barrier, inc=1, device_id=(z - 1, t), device_id_type=MESH)

    @pl.when(z < n - 1)
    def _():
        pl.semaphore_signal(barrier, inc=1, device_id=(z + 1, t), device_id_type=MESH)

    def greet(k, carry):
        peer = lax.rem(t + k, width)
        pl.semaphore_signal(barrier, inc=1, device_id=(z, peer), device_id_type=MESH)
        return carry

    lax.fori_loop(1, width, greet, 0)
    pl.semaphore_wait(barrier, jnp.where(is_end, width, width + 1))

    def chain_copy(d, c):
        return pltpu.make_async_remote_copy(
            src_ref=partial.at[d, c],
            dst_ref=arrived.at[d, c],
            send_sem=chain_send.at[d, c],
            recv_sem=chain_recv.at[d, c],
            device_id=(z + 2 * d - 1, t),
            device_id_type=MESH,
        )

    def own(d, c):
        block = d * half + c
        moment = m_ref[slot[block]].astype(jnp.float32)
        return g_ref[block].astype(jnp.float32) + weight[block] * moment

    def my_rows(place):
        return pl.ds(pl.multiple_of(place * rows, rows), rows)

    def start_chain(d, c):
        partial[d, c] = own(d, c).astype(jnp.bfloat16)
        chain_copy(d, c).start()

    def add_chain(d, c):
        chain_copy(d, c).wait_recv()
        total = own(d, c) + arrived[d, c].astype(jnp.float32)
        partial[d, c] = total.astype(jnp.bfloat16)

    def scatter_copy(d, c, peer, sem):
        return pltpu.make_async_remote_copy(
            src_ref=partial.at[d, c],
            dst_ref=whole.at[c // width, my_rows(t)],
            send_sem=scatter_send.at[c],
            recv_sem=sem,
            device_id=(z, peer),
            device_id_type=MESH,
        )

    def return_copy(d, j, peer):
        block = d * half + j * width + t
        return pltpu.make_async_remote_copy(
            src_ref=ready.at[j, my_rows(peer)],
            dst_ref=gathered.at[block],
            send_sem=return_send.at[j, peer],
            recv_sem=gather_recv.at[block],
            device_id=(z, peer),
            device_id_type=MESH,
        )

    def ahead_copy(d, c):
        block = d * half + c
        return pltpu.make_async_remote_copy(
            src_ref=gathered.at[block],
            dst_ref=gathered.at[block],
            send_sem=ahead_send.at[block],
            recv_sem=gather_recv.at[block],
            device_id=(z + 1 - 2 * d, t),
            device_id_type=MESH,
        )

    def pass_on(d, c):
        ahead_copy(d, c).wait_recv()

        @pl.when((z + 1 - 2 * d >= 0) & (z + 1 - 2 * d < n))
        def _():
            ahead_copy(d, c).start()

    def iterate_in(j):
        widened = whole[j].astype(jnp.float32) * (1.0 + decay_rate)
        length = jnp.sqrt(jnp.sum(widened * widened)) + norm_eps
        current[...] = widened / length

        def once(k, carry):
            now = current[...]
            low_now = now.astype(jnp.bfloat16)
            squared = lax.dot_general(
                low_now, low_now, (((1,), (1,)), ((), ())), preferred_element_type=jnp.float32
            )
            low_squared = squared.astype(jnp.bfloat16)
            polynomial = newton_b * squared + newton_c * jnp.dot(
                low_squared, low_squared, preferred_element_type=jnp.float32
            )
            current[...] = newton_a * now + jnp.dot(
                polynomial.astype(jnp.bfloat16), low_now, preferred_element_type=jnp.float32
            )
            return carry

        lax.fori_loop(0, ITERS, once, 0)
        ready[j] = (current[...] * math.sqrt(columns)).astype(jnp.bfloat16)

    @pl.when(is_end)
    def _():
        near = jnp.where(z == 0, 0, 1)
        far = 1 - near

        def begin(c, carry):
            start_chain(far, c)
            return carry

        lax.fori_loop(0, half, begin, 0)

        def pass_group(j):
            def one(k, inner):
                pass_on(near, j * width + k)
                return inner

            lax.fori_loop(0, width, one, 0)

        def reduce_group(j):
            def chunk(k, inner):
                c = j * width + k
                add_chain(near, c)

                @pl.when(k == t)
                def _():
                    pltpu.make_async_copy(
                        partial.at[near, c], whole.at[j, my_rows(t)], scatter_recv.at[j, t]
                    ).start()

                @pl.when(k != t)
                def _():
                    scatter_copy(near, c, k, scatter_recv.at[j, t]).start()

                return inner

            lax.fori_loop(0, width, chunk, 0)

        def iterate_group(j):
            def land(k, inner):
                pltpu.make_async_copy(
                    partial.at[near, 0], whole.at[j, my_rows(k)], scatter_recv.at[j, k]
                ).wait()
                return inner

            lax.fori_loop(0, width, land, 0)
            iterate_in(j)

            def give(k, inner):
                @pl.when(k == t)
                def _():
                    block = near * half + j * width + t
                    pltpu.make_async_copy(
                        ready.at[j, my_rows(t)], gathered.at[block], gather_recv.at[block]
                    ).start()

                @pl.when(k != t)
                def _():
                    return_copy(near, j, k).start()

                return inner

            lax.fori_loop(0, width, give, 0)

        def block_step(j, carry):
            @pl.when(j < per_device)
            def _():
                reduce_group(j)

            @pl.when(j > 1)
            def _():
                pass_group(j - 2)

            @pl.when(j > 0)
            def _():
                iterate_group(j - 1)

            return carry

        lax.fori_loop(0, per_device + 1, block_step, 0)
        pass_group(per_device - 1)

        def finish(c, carry):
            pass_on(far, c)
            return carry

        lax.fori_loop(0, half, finish, 0)

    @pl.when(jnp.logical_not(is_end))
    def _():
        early = jnp.where(low, 1, 0)

        def forward(d, c):
            add_chain(d, c)
            chain_copy(d, c).start()

        def step(i, carry):
            @pl.when(i < half)
            def _():
                forward(early, i)

            @pl.when((i >= lead) & (i < half + lead))
            def _():
                forward(1 - early, i - lead)

            @pl.when((i >= gap) & (i < half + gap))
            def _():
                pass_on(1 - early, i - gap)

            @pl.when(i >= gap + lead)
            def _():
                pass_on(early, i - gap - lead)

            return carry

        lax.fori_loop(0, half + gap + lead, step, 0)

    final = pltpu.make_async_copy(gathered, out_ref, out_sem)
    final.start()

    for d in range(2):
        sink = 0 if d == 0 else n - 1

        def settle(c, carry):
            @pl.when(z != sink)
            def _():
                chain_copy(d, c).wait_send()

            @pl.when(z != n - 1 - sink)
            def _():
                ahead_copy(d, c).wait_send()

            @pl.when((z == sink) & (lax.rem(c, width) != t))
            def _():
                scatter_copy(d, c, lax.rem(c, width), scatter_recv.at[0, 0]).wait_send()
                return_copy(d, c // width, lax.rem(c, width)).wait_send()

            return carry

        lax.fori_loop(0, half, settle, 0)
    final.wait()


def pick_kernel(group, index, filled, in_ref, out_ref):
    base = pl.program_id(0) * group
    for k in range(group):
        piece = in_ref[index[base + k]].astype(jnp.float32)
        out_ref[0, k] = jnp.where(filled[base + k] > 0, piece, jnp.zeros_like(piece))


def fused(gradients, momentum, owners):
    n = lax.axis_size("dp")
    width = lax.axis_size("tensor")
    me = lax.axis_index("dp")
    pieces = gradients[0]
    blocks_all, rows, columns = pieces.shape
    capacity = momentum.shape[1]
    half = blocks_all // 2
    lead = min(2, half)
    slot_rank = ranks_of(owners)
    mine = owners == me
    ratio = decay_rate * decay_rate / (1.0 + decay_rate)
    weight = jnp.where(mine, ratio, 0.0).astype(jnp.float32)
    slot = jnp.minimum(slot_rank, capacity - 1)
    order = columns
    low = jnp.bfloat16
    all_results = pl.pallas_call(
        functools.partial(kernel, (n, width, half, rows, lead)),
        out_shape=jax.ShapeDtypeStruct((blocks_all, rows, columns), low),
        in_specs=[
            pl.BlockSpec(memory_space=pltpu.SMEM),
            pl.BlockSpec(memory_space=pltpu.SMEM),
            pl.BlockSpec(memory_space=pltpu.VMEM),
            pl.BlockSpec(memory_space=pltpu.VMEM),
        ],
        out_specs=pl.BlockSpec(memory_space=pl.ANY),
        scratch_shapes=[
            pltpu.VMEM((2, half, rows, columns), low),
            pltpu.VMEM((2, half, rows, columns), low),
            pltpu.VMEM((half // width, order, columns), low),
            pltpu.VMEM((half // width, order, columns), low),
            pltpu.VMEM((blocks_all, rows, columns), low),
            pltpu.VMEM((order, columns), jnp.float32),
            pltpu.SemaphoreType.DMA((2, half)),
            pltpu.SemaphoreType.DMA((2, half)),
            pltpu.SemaphoreType.DMA((half,)),
            pltpu.SemaphoreType.DMA((half // width, width)),
            pltpu.SemaphoreType.DMA((half // width, width)),
            pltpu.SemaphoreType.DMA((blocks_all,)),
            pltpu.SemaphoreType.DMA((blocks_all,)),
            pltpu.SemaphoreType.DMA,
        ],
        compiler_params=pltpu.CompilerParams(
            collective_id=0, has_side_effects=True, vmem_limit_bytes=50 * 1024 * 1024
        ),
        name="muon_chain",
    )(weight, slot, pieces, momentum[0])

    slot_ids = jnp.arange(capacity, dtype=jnp.int32)
    places = jnp.arange(blocks_all, dtype=jnp.int32)
    my_slots = mine[:, None] & (slot_rank[:, None] == slot_ids[None, :])
    filled = jnp.any(my_slots, axis=0).astype(jnp.int32)
    index = jnp.sum(jnp.where(my_slots, places[:, None], 0), axis=0)
    group = math.gcd(capacity, 4)
    return pl.pallas_call(
        functools.partial(pick_kernel, group),
        out_shape=jax.ShapeDtypeStruct((1, capacity, rows, columns), jnp.float32),
        grid_spec=pltpu.PrefetchScalarGridSpec(
            num_scalar_prefetch=2,
            grid=(capacity // group,),
            in_specs=[pl.BlockSpec(memory_space=pltpu.VMEM)],
            out_specs=pl.BlockSpec((1, group, rows, columns), lambda s, index, filled: (0, s, 0, 0)),
        ),
        name="muon_pick",
    )(index, filled, all_results)


def choose(gradients, momentum, owners):
    n, width = lax.axis_size("dp"), lax.axis_size("tensor")
    blocks_all = gradients.shape[1]
    if n > 1 and blocks_all % (2 * width) == 0 and gradients.shape[2] % 16 == 0:
        return fused(gradients, momentum, owners)
    return body(gradients, momentum, owners)


def solution(mesh):
    in_specs = (P("dp", None, "tensor", None), P("dp", None, "tensor", None), P())
    out_specs = P("dp", None, "tensor", None)
    return jax.shard_map(choose, mesh=mesh, in_specs=in_specs, out_specs=out_specs, check_vma=False)
```
